32 devices in a mesh: rows: 2 (over core), sites: 4 (over z), bond: 4 (over y, x).
Axes of the slice: x: 2, y: 2, z: 4, core: 2. Of those that a mesh axis runs over, the one named last changes fastest.
Arguments:
- boundary_in: float32 [1, 4, 256, 8, 256], P(None, 'sites', None, None, 'bond'), may hold values from -6 to 6
- mpo: float32 [4, 4, 8, 8, 8, 8], P('rows', 'sites'), may hold values from -0.75 to 0.75
- proj: float32 [4, 4, 256, 8, 256], P('rows', 'sites'), may hold values from -0.125 to 0.125
Outputs:
- boundary_out: float32 [2, 1, 4, 256, 8, 256], P('rows', None, 'sites', None, None, 'bond')
The draws below stay inside these ranges and needn't reach their ends.
All inputs are finite; a program needn't handle non-finite values.
Results may differ from the reference program's by a relative error of at most 0.00013.
Values sent between devices are 32-bit elements; how exact they have to be, the bound alone decides.
No kernel may reach another device: no remote copies, remote signals or barrier semaphores. Data moves between devices by JAX's collectives and lax.ppermute only.
A program may use at most 64 MiB of HBM per device.

```python
import jax
import jax.numpy as jnp
from jax import lax

CHI = 256
DB = 8
TERMS = 1
GROUP_ROWS = 2
SITES = 4
LROWS = 4
N_ROWS = 2


def levels(own_key, shape, pieces, least, top_value):
    level = 1.0
    for position, parts in pieces:
        steps = jax.random.uniform(jax.random.fold_in(jax.random.fold_in(own_key, 6), position), (parts,), jnp.float32, least / len(pieces), top_value / len(pieces))
        level = level * jnp.repeat(jnp.exp(steps), shape[position] // parts).reshape((-1,) + (1,) * (len(shape) - 1 - position))
    return level


def bell_draw(own_key, dims, spread, bound, split=(), dtype=jnp.bfloat16):
    gain = levels(own_key, dims, split, -0.22, 0.18) if split else 1.0
    result = jax.random.normal(own_key, dims, jnp.float32) * spread * gain
    return jnp.minimum(jnp.maximum(result, -bound), bound).astype(dtype)


def setup_inputs(seed: int = 0) -> dict:
    seeds = jax.random.split(jax.random.key(seed), 4)
    boundary_in = bell_draw(seeds[0], (TERMS, SITES, CHI, DB, CHI), 1.0, 6.0, ((1, 4), (4, 4)), jnp.float32)
    mpo = bell_draw(seeds[1], (LROWS, SITES, DB, DB, DB, DB), (DB * DB) ** -0.5, 0.75, ((0, 2), (1, 4)), jnp.float32)
    proj = bell_draw(seeds[2], (LROWS, SITES, CHI, DB, CHI), (CHI * DB) ** -0.5, 0.125, ((0, 2), (1, 4)), jnp.float32)
    return dict(boundary_in=boundary_in, mpo=mpo, proj=proj)


def absorb_site(packed):
    boundary, left_proj, mpo_row, right_proj = packed
    precise = lax.Precision.HIGHEST
    left_part = jnp.einsum('alx,taub->tlxub', left_proj, boundary, precision=precise)
    mixed_rows = jnp.einsum('tlxub,ludr->txdbr', left_part, mpo_row, precision=precise)
    return jnp.einsum('txdbr,bry->txdy', mixed_rows, right_proj, precision=precise)

def reference(boundary_in, mpo, proj):
    current = jnp.moveaxis(boundary_in, 1, 0)
    results = []
    for group_pos in range(N_ROWS):
        for inner_row in range(GROUP_ROWS):
            lattice_row = GROUP_ROWS * group_pos + inner_row
            right_proj = proj[lattice_row]
            left_proj = jnp.roll(right_proj, 1, axis=0)
            current = lax.map(absorb_site, (current, left_proj, mpo[lattice_row], right_proj))
        square_sum = lax.optimization_barrier(jnp.sum(current * current, axis=(2, 3, 4), keepdims=True))
        current = current / jnp.sqrt(square_sum / (CHI * DB * CHI) + 1e-06)
        results.append(jnp.moveaxis(current, 0, 1))
    return jnp.stack(results)
```

```python
import functools

import jax
import jax.numpy as jnp
from jax import lax
from jax.experimental import pallas as pl
from jax.experimental.pallas import tpu as pltpu
from jax.sharding import PartitionSpec as P

f32, bf16 = jnp.float32, jnp.bfloat16
LANES = 128
EPS = 1e-06
MIB = 2**20


def split(value):
    high = value.astype(bf16)
    return high, (value - high.astype(f32)).astype(bf16)


def dot(left, right):
    return jnp.dot(left, right, preferred_element_type=f32)


def swap_cores(value):
    return lax.ppermute(value, "rows", [(0, 1), (1, 0)])


def from_peer(value, k, n):
    if n & (n - 1) == 0:
        pairs = [(i, i ^ k) for i in range(n)]
    else:
        pairs = [((i + k) % n, i) for i in range(n)]
    return lax.ppermute(value, "bond", pairs)


def peer(j, k, n):
    return j ^ k if n & (n - 1) == 0 else lax.rem(j + k, n)


def row_kernel(cfg, *refs):
    n, first, stats, do_a, do_b, row, bond, phys, group_rows = cfg
    half = bond // 2
    width = bond // n
    step = half // n
    rows_half = half * phys
    refs = list(refs)
    scal = refs.pop(0)
    if do_a:
        if first:
            pieces = [refs.pop(0) for _ in range(n)]
        else:
            keep_in, recv_in = refs.pop(0), refs.pop(0)
        own, other, mats = refs.pop(0), refs.pop(0), refs.pop(0)
    else:
        tp = refs.pop(0)
    if do_b:
        lefts = [refs.pop(0) for _ in range(n)]
    if do_a and not do_b:
        tp = refs.pop(0)
    if do_b:
        keep, send = refs.pop(0), refs.pop(0)
    if stats:
        full_out, sum_out = refs.pop(0), refs.pop(0)
    if do_a and do_b:
        tp = refs.pop(0)
    if do_a:
        bs, bh, rbuf, rc, th, sem = (refs.pop(0) for _ in range(6))
    if do_b:
        lh = refs.pop(0)
    core = scal[0]
    j = scal[1]

    if do_a:
        source, slot = row // group_rows, row % group_rows
        lanes = [slice(h * LANES, (h + 1) * LANES) for h in range(bond // LANES)]

        def copies(ref):
            return [pltpu.make_async_copy(ref.at[slot, :, lane], rbuf.at[h], sem.at[h]) for h, lane in enumerate(lanes)]

        @pl.when(core == source)
        def _():
            for copy in copies(own):
                copy.start()

        @pl.when(core != source)
        def _():
            for copy in copies(other):
                copy.start()

        if first:
            pack = LANES // width
            group = rows_half // pack
            for k in range(n):
                for g in range(pack):
                    bs[g * group:(g + 1) * group, k * width:(k + 1) * width] = pieces[k][:, g * width:(g + 1) * width]
        else:
            for h, lane in enumerate(lanes):
                bs[:, lane] = keep_in[h] + recv_in[h]
        if stats:
            full = bs[...]
            for h, lane in enumerate(lanes):
                full_out[h] = full[:, lane]
            sum_out[...] = jnp.full(sum_out.shape, jnp.sum(full * full), f32)
        block = step * phys
        for k in range(n):
            at = pl.multiple_of(peer(j, k, n) * block, block)
            high, low = split(bs[pl.ds(at, block), :])
            into = slice(k * block, (k + 1) * block)
            bh[into, 0:bond] = high
            bh[into, bond:2 * bond] = high
            bh[into, 2 * bond:3 * bond] = low
        for copy in copies(own):
            copy.wait()
        for q in range(phys):
            for k in range(n if first else 1):
                if first:
                    rows = width
                    at = peer(j, k, n) * (width * phys) + q
                else:
                    rows = bond
                    at = q
                for h, lane in enumerate(lanes):
                    high, low = split(rbuf[h, pl.ds(at, rows, stride=phys), :])
                    for part, piece in enumerate((high, low, high)):
                        lo = part * bond + k * rows
                        rc[q, lo:lo + rows, lane] = piece

        count = th.shape[0]
        block = count * phys

        def chunk(i, carry):
            lines = bh[pl.ds(pl.multiple_of(i * block, block), block), :]
            for p in range(phys // 2):
                pair = [dot(lines, rc[2 * p + s]).reshape(count, phys, bond) for s in range(2)]
                high, low = split(jnp.concatenate(pair, axis=1))
                size = 2 * phys
                th[:, p * size:(p + 1) * size, :] = high
                th[:, phys * phys + p * size:phys * phys + (p + 1) * size, :] = low
            unroll = min(16, count // 2)

            def mix(m, inner):
                for u in range(unroll):
                    kk = m * unroll + u
                    pair = []
                    for s in range(2):
                        got = dot(mats[...], th[2 * kk + s])
                        got = got[:phys * phys] + got[phys * phys:]
                        pair.append(got.reshape(phys, phys, bond))
                    high, low = split(jnp.concatenate(pair, axis=1))
                    at = pl.multiple_of(i * block + kk * (2 * phys), 2 * phys)
                    for d in range(phys):
                        tp[0, d, pl.ds(at, 2 * phys), :] = high[d]
                        tp[1, d, pl.ds(at, 2 * phys), :] = low[d]
                return inner

            return lax.fori_loop(0, count // 2 // unroll, mix, carry)

        lax.fori_loop(0, half // count, chunk, 0)

    if do_b:
        block = step * phys
        for k in range(n):
            for side in range(2):
                which = core if side == 0 else 1 - core
                value = lefts[k][pl.ds(pl.multiple_of(which * half, half), half), :]
                high, low = split(value)
                into = slice(side * half, (side + 1) * half)
                for part, piece in enumerate((high, low, high)):
                    lh[into, part * rows_half + k * block:part * rows_half + (k + 1) * block] = piece
        for d in range(phys):
            right = jnp.concatenate([tp[0, d], tp[0, d], tp[1, d]], axis=0)
            total = dot(lh[...], right)
            for h in range(bond // LANES):
                lane = slice(h * LANES, (h + 1) * LANES)
                keep[h, pl.ds(d, half, stride=phys), :] = total[:half, lane]
                send[h, pl.ds(d, half, stride=phys), :] = total[half:, lane]


def row_call(cfg, scal, ins):
    n, first, stats, do_a, do_b, row, bond, phys, group_rows = cfg
    half = bond // 2
    rows_half = half * phys
    count = min(64, half)
    vmem, any_, smem = pltpu.VMEM, pl.ANY, pltpu.SMEM
    spaces = [smem]
    if do_a:
        spaces += [vmem] * (n if first else 2) + [any_, any_, vmem]
    else:
        spaces += [vmem]
    if do_b:
        spaces += [vmem] * n
    tp_shape = (2, phys, rows_half, bond)
    outs = []
    if do_a and not do_b:
        outs.append(jax.ShapeDtypeStruct(tp_shape, bf16))
    if do_b:
        outs += [jax.ShapeDtypeStruct((bond // LANES, rows_half, LANES), f32)] * 2
    if stats:
        outs += [jax.ShapeDtypeStruct((bond // LANES, rows_half, LANES), f32), jax.ShapeDtypeStruct((8, LANES), f32)]
    scratch = []
    if do_a and do_b:
        scratch.append(vmem(tp_shape, bf16))
    if do_a:
        scratch += [
            vmem((rows_half, bond), f32),
            vmem((rows_half, 3 * bond), bf16),
            vmem((bond // LANES, bond * phys, LANES), f32),
            vmem((phys, 3 * bond, bond), bf16),
            vmem((count, 2 * phys * phys, bond), bf16),
            pltpu.SemaphoreType.DMA((bond // LANES,)),
        ]
    if do_b:
        scratch.append(vmem((bond, 3 * rows_half), bf16))
    flops = (do_a * 2 + do_b) * 3 * 2 * rows_half * bond * bond * phys
    return pl.pallas_call(
        functools.partial(row_kernel, cfg),
        out_shape=outs,
        in_specs=[pl.BlockSpec(memory_space=s) for s in spaces],
        out_specs=[pl.BlockSpec(memory_space=vmem)] * len(outs),
        scratch_shapes=scratch,
        compiler_params=pltpu.CompilerParams(vmem_limit_bytes=40 * MIB),
        cost_estimate=pl.CostEstimate(flops=flops, bytes_accessed=4 * MIB, transcendentals=0),
        name=f"row{row}{'a' if do_a else ''}{'b' if do_b else ''}",
    )(scal, *ins)


def scale_of(total, entries):
    return 1.0 / jnp.sqrt(total / entries + EPS)


def sum_kernel(entries, n, width, scal, keep, recv, first_full, sum_mine, sum_theirs, fin_keep, fin_send, sum_out):
    core = scal[0]
    near = lax.div(scal[1] * width, LANES)
    scale = scale_of(sum_mine[0:1, 0:1] + sum_theirs[0:1, 0:1], entries)
    rows = keep.shape[1]
    value = (keep[...] + recv[...]) * jnp.broadcast_to(scale, keep.shape)
    sum_out[...] = jnp.full(sum_out.shape, jnp.sum(value * value), f32)
    spread = jnp.broadcast_to(scale, (rows, LANES))
    last = (keep[near] + recv[near]) * spread
    early = first_full[near] * spread

    @pl.when(core == 0)
    def _():
        fin_keep[...] = early
        fin_send[...] = last

    @pl.when(core != 0)
    def _():
        fin_keep[...] = last
        fin_send[...] = early


def final_kernel(entries, n, width, scal, fin_keep, fin_recv, sum_mine, sum_theirs, out):
    core = scal[0]
    shift = lax.rem(LANES - lax.rem(scal[1] * width, LANES), LANES)
    rows = fin_keep.shape[0]
    scale = scale_of(sum_mine[0:1, 0:1] + sum_theirs[0:1, 0:1], entries)
    scale = jnp.where(core == 0, 1.0, jnp.broadcast_to(scale, (rows, LANES)))
    mine = pltpu.roll(fin_keep[...] * scale, shift, 1)[:, :width]
    theirs = pltpu.roll(fin_recv[...] * scale, shift, 1)[:, :width]
    out[pl.ds(pl.multiple_of(core * rows, rows), rows), :] = mine
    out[pl.ds(pl.multiple_of((1 - core) * rows, rows), rows), :] = theirs


def small_call(kernel, name, outs, scal, *ins):
    vmem = pltpu.VMEM
    return pl.pallas_call(
        kernel,
        out_shape=outs,
        in_specs=[pl.BlockSpec(memory_space=pltpu.SMEM)] + [pl.BlockSpec(memory_space=vmem)] * len(ins),
        out_specs=[pl.BlockSpec(memory_space=vmem)] * len(outs),
        compiler_params=pltpu.CompilerParams(vmem_limit_bytes=20 * MIB),
        name=name,
    )(scal, *ins)


def body(boundary_in, mpo, proj):
    bond, phys, width = boundary_in.shape[2:]
    n = lax.axis_size("bond")
    sites = lax.axis_size("sites")
    groups = lax.axis_size("rows")
    group_rows = proj.shape[0]
    core = lax.axis_index("rows")
    j = lax.axis_index("bond")
    half = bond // 2
    step = half // n
    entries = bond * phys * bond
    scal = jnp.stack([core, j]).astype(jnp.int32)

    own = proj[:, 0]

    def slices(which):
        got = lax.dynamic_slice_in_dim(own, which * half + j * step, step, 1)
        return jnp.swapaxes(got.reshape(group_rows, step * phys, bond), 1, 2)

    got = swap_cores(slices(1 - core))
    mine = slices(core)

    start = lax.dynamic_slice_in_dim(boundary_in[0, 0], core * half, half, 0)
    pack = LANES // width
    start = start.reshape(pack, half // pack, phys, width)
    start = jnp.concatenate([start[g] for g in range(pack)], axis=-1).reshape(half // pack * phys, LANES)
    pieces = [start] + [from_peer(start, k, n) for k in range(1, n)]

    other = swap_cores(own)
    mpo_own = mpo[:, 0]
    mpo_other = swap_cores(mpo_own)

    flat = (group_rows, bond * phys, bond)
    own_flat, other_flat = own.reshape(flat), other.reshape(flat)

    def pick(row, own_value, other_value):
        source, slot = divmod(row, group_rows)
        return jnp.where(core == source, own_value[slot], other_value[slot])

    def mix_matrix(row):
        value = pick(row, mpo_own, mpo_other)
        value = jnp.transpose(value, (2, 0, 3, 1)).reshape(phys * phys, phys * phys)
        high = lax.reduce_precision(value, 8, 7)
        low = (value - high).astype(bf16)
        high = high.astype(bf16)
        return jnp.concatenate([jnp.concatenate([high, high], 1), jnp.concatenate([low, low], 1)], 0)

    ring = [(i, (i + 1) % sites) for i in range(sites)]
    batches = [[0], [1], list(range(2, groups * group_rows))]
    lefts = {}
    for rows in batches:
        value = jnp.stack([pick(r, mine, got) for r in rows])
        value = lax.ppermute(value, "sites", ring)
        parts = [value] + [from_peer(value, k, n) for k in range(1, n)]
        for position, r in enumerate(rows):
            lefts[r] = [part[position] for part in parts]

    keep = recv = None
    for row in range(groups * group_rows):
        first, stats = row == 0, row == group_rows
        base = (n, first, stats, True, True, row, bond, phys, group_rows)
        entry = pieces if first else [keep, recv]
        entry = entry + [own_flat, other_flat, mix_matrix(row)]
        if first:
            (mixed,) = row_call(base[:4] + (False,) + base[5:], scal, entry)
            keep, send = row_call(base[:3] + (False, True) + base[5:], scal, [mixed] + lefts[row])
        else:
            result = row_call(base, scal, entry + lefts[row])
            keep, send = result[:2]
            if stats:
                full, sum_first = result[2:]
                sum_first_other = swap_cores(sum_first)
        recv = swap_cores(send)
    rows_half = half * phys
    block = jax.ShapeDtypeStruct((rows_half, LANES), f32)
    fin_keep, fin_send, sum_last = small_call(
        functools.partial(sum_kernel, entries, n, width),
        "sums",
        [block, block, jax.ShapeDtypeStruct((8, LANES), f32)],
        scal, keep, recv, full, sum_first, sum_first_other,
    )
    (out,) = small_call(
        functools.partial(final_kernel, entries, n, width),
        "final",
        [jax.ShapeDtypeStruct((bond * phys, width), f32)],
        scal, fin_keep, swap_cores(fin_send), sum_last, swap_cores(sum_last),
    )
    return out.reshape(1, 1, 1, bond, phys, width)


def solution(mesh):
    return jax.shard_map(
        body,
        mesh=mesh,
        in_specs=(
            P(None, "sites", None, None, "bond"),
            P("rows", "sites", None, None, None, None),
            P("rows", "sites", None, None, None),
        ),
        out_specs=P("rows", None, "sites", None, None, "bond"),
        check_vma=False,
    )
```

```python
import functools

import jax
import jax.numpy as jnp
from jax import lax
from jax.experimental import pallas as pl
from jax.experimental.pallas import tpu as pltpu
from jax.sharding import PartitionSpec as P


f32, bf16 = jnp.float32, jnp.bfloat16
LANES = 128
EPS = 1e-06
MIB = 2**20


def split(value):
    high = value.astype(bf16)
    return high, (value - high.astype(f32)).astype(bf16)


def dot(left, right):
    return jnp.dot(left, right, preferred_element_type=f32)


def swap_cores(value):
    return lax.ppermute(value, "rows", [(0, 1), (1, 0)])


def from_peer(value, k, n):
    if n & (n - 1) == 0:
        pairs = [(i, i ^ k) for i in range(n)]
    else:
        pairs = [((i + k) % n, i) for i in range(n)]
    return lax.ppermute(value, "bond", pairs)


def peer(j, k, n):
    return j ^ k if n & (n - 1) == 0 else lax.rem(j + k, n)


def row_kernel(cfg, *refs):
    n, first, stats, do_a, do_b, row, bond, phys, group_rows, place = cfg
    half = bond // 2
    width = bond // n
    step = half // n
    rows_half = half * phys
    refs = list(refs)
    scal = refs.pop(0)
    if do_a:
        if first:
            pieces = [refs.pop(0) for _ in range(n)]
        else:
            keep_in, recv_in = refs.pop(0), refs.pop(0)
        own, other, mats = refs.pop(0), refs.pop(0), refs.pop(0)
    else:
        tp = refs.pop(0)
    if do_b:
        lefts = [refs.pop(0) for _ in range(n)]
    if do_a and not do_b:
        tp = refs.pop(0)
    if do_b:
        keep, send = refs.pop(0), refs.pop(0)
    if stats:
        full_out, sum_out = refs.pop(0), refs.pop(0)
    if do_a and do_b:
        tp = refs.pop(0)
    if do_a:
        bs, bh, rbuf, rc, th, sem = (refs.pop(0) for _ in range(6))
    if do_b:
        lh = refs.pop(0)
    core = scal[0]
    j = scal[1]

    if do_a:
        source, slot = row // group_rows, row % group_rows
        lanes = [slice(h * LANES, (h + 1) * LANES) for h in range(bond // LANES)]

        def copies(ref):
            return [pltpu.make_async_copy(ref.at[slot, :, lane], rbuf.at[h], sem.at[h]) for h, lane in enumerate(lanes)]

        @pl.when(core == source)
        def _():
            for copy in copies(own):
                copy.start()

        @pl.when(core != source)
        def _():
            for copy in copies(other):
                copy.start()

        if first:
            pack = LANES // width
            group = rows_half // pack
            for k in range(n):
                for g in range(pack):
                    bs[g * group:(g + 1) * group, k * width:(k + 1) * width] = pieces[k][:, g * width:(g + 1) * width]
        else:
            for h, lane in enumerate(lanes):
                bs[:, lane] = keep_in[h] + recv_in[h]
        if stats:
            full = bs[...]
            for h, lane in enumerate(lanes):
                full_out[h] = full[:, lane]
            sum_out[...] = jnp.full(sum_out.shape, jnp.sum(full * full), f32)
        block = step * phys
        for k in range(n):
            at = pl.multiple_of(peer(j, k, n) * block, block)
            high, low = split(bs[pl.ds(at, block), :])
            into = slice(k * block, (k + 1) * block)
            bh[into, 0:bond] = high
            bh[into, bond:2 * bond] = high
            bh[into, 2 * bond:3 * bond] = low
        for copy in copies(own):
            copy.wait()
        for q in range(phys):
            for k in range(n if first else 1):
                if first:
                    rows = width
                    at = peer(j, k, n) * (width * phys) + q
                else:
                    rows = bond
                    at = q
                for h, lane in enumerate(lanes):
                    high, low = split(rbuf[h, pl.ds(at, rows, stride=phys), :])
                    for part, piece in enumerate((high, low, high)):
                        lo = part * bond + k * rows
                        rc[q, lo:lo + rows, lane] = piece

        count = th.shape[0]
        block = count * phys

        def chunk(i, carry):
            lines = bh[pl.ds(pl.multiple_of(i * block, block), block), :]
            for p in range(phys // 2):
                pair = [dot(lines, rc[2 * p + s]).reshape(count, phys, bond) for s in range(2)]
                high, low = split(jnp.concatenate(pair, axis=1))
                size = 2 * phys
                th[:, p * size:(p + 1) * size, :] = high
                th[:, phys * phys + p * size:phys * phys + (p + 1) * size, :] = low
            unroll = min(16, count // 2)

            def mix(m, inner):
                for u in range(unroll):
                    kk = m * unroll + u
                    pair = []
                    for s in range(2):
                        got = dot(mats[row], th[2 * kk + s])
                        got = got[:phys * phys] + got[phys * phys:]
                        pair.append(got.reshape(phys, phys, bond))
                    high, low = split(jnp.concatenate(pair, axis=1))
                    at = pl.multiple_of(i * block + kk * (2 * phys), 2 * phys)
                    for d in range(phys):
                        tp[0, d, pl.ds(at, 2 * phys), :] = high[d]
                        tp[1, d, pl.ds(at, 2 * phys), :] = low[d]
                return inner

            return lax.fori_loop(0, count // 2 // unroll, mix, carry)

        lax.fori_loop(0, half // count, chunk, 0)

    if do_b:
        block = step * phys
        for k in range(n):
            for side in range(2):
                which = core if side == 0 else 1 - core
                value = lefts[k][place, pl.ds(pl.multiple_of(which * half, half), half), :]
                high, low = split(value)
                into = slice(side * half, (side + 1) * half)
                for part, piece in enumerate((high, low, high)):
                    lh[into, part * rows_half + k * block:part * rows_half + (k + 1) * block] = piece
        for d in range(phys):
            right = jnp.concatenate([tp[0, d], tp[0, d], tp[1, d]], axis=0)
            total = dot(lh[...], right)
            for h in range(bond // LANES):
                lane = slice(h * LANES, (h + 1) * LANES)
                keep[h, pl.ds(d, half, stride=phys), :] = total[:half, lane]
                send[h, pl.ds(d, half, stride=phys), :] = total[half:, lane]


def row_call(cfg, scal, ins):
    n, first, stats, do_a, do_b, _, bond, phys, _, _ = cfg
    half = bond // 2
    rows_half = half * phys
    count = min(64, half)
    vmem, any_, smem = pltpu.VMEM, pltpu.HBM, pltpu.SMEM
    spaces = [smem]
    if do_a:
        spaces += [vmem] * (n if first else 2) + [any_, any_, vmem]
    else:
        spaces += [vmem]
    if do_b:
        spaces += [vmem] * n
    tp_shape = (2, phys, rows_half, bond)
    outs = []
    if do_a and not do_b:
        outs.append(jax.ShapeDtypeStruct(tp_shape, bf16))
    if do_b:
        outs += [jax.ShapeDtypeStruct((bond // LANES, rows_half, LANES), f32)] * 2
    if stats:
        outs += [jax.ShapeDtypeStruct((bond // LANES, rows_half, LANES), f32), jax.ShapeDtypeStruct((8, LANES), f32)]
    scratch = []
    if do_a and do_b:
        scratch.append(vmem(tp_shape, bf16))
    if do_a:
        scratch += [
            vmem((rows_half, bond), f32),
            vmem((rows_half, 3 * bond), bf16),
            vmem((bond // LANES, bond * phys, LANES), f32),
            vmem((phys, 3 * bond, bond), bf16),
            vmem((count, 2 * phys * phys, bond), bf16),
            pltpu.SemaphoreType.DMA((bond // LANES,)),
        ]
    if do_b:
        scratch.append(vmem((bond, 3 * rows_half), bf16))
    flops = (do_a * 2 + do_b) * 3 * 2 * rows_half * bond * bond * phys
    return pl.pallas_call(
        functools.partial(row_kernel, cfg),
        out_shape=outs,
        in_specs=[pl.BlockSpec(memory_space=s) for s in spaces],
        out_specs=[pl.BlockSpec(memory_space=vmem)] * len(outs),
        scratch_shapes=scratch,
        compiler_params=pltpu.CompilerParams(vmem_limit_bytes=30 * MIB),
        cost_estimate=pl.CostEstimate(flops=flops, bytes_accessed=4 * MIB, transcendentals=0),
    )(scal, *ins)


def scale_of(total, entries):
    return 1.0 / jnp.sqrt(total / entries + EPS)


def sum_kernel(entries, width, scal, keep, recv, first_full, sum_mine, sum_theirs, fin_keep, fin_send, sum_out):
    core = scal[0]
    near = lax.div(scal[1] * width, LANES)
    scale = scale_of(sum_mine[0:1, 0:1] + sum_theirs[0:1, 0:1], entries)
    rows = keep.shape[1]
    value = (keep[...] + recv[...]) * jnp.broadcast_to(scale, keep.shape)
    sum_out[...] = jnp.full(sum_out.shape, jnp.sum(value * value), f32)
    spread = jnp.broadcast_to(scale, (rows, LANES))
    last = (keep[near] + recv[near]) * spread
    early = first_full[near] * spread

    @pl.when(core == 0)
    def _():
        fin_keep[...] = early
        fin_send[...] = last

    @pl.when(core != 0)
    def _():
        fin_keep[...] = last
        fin_send[...] = early


def final_kernel(entries, width, scal, fin_keep, fin_recv, sum_mine, sum_theirs, out):
    core = scal[0]
    shift = lax.rem(LANES - lax.rem(scal[1] * width, LANES), LANES)
    rows = fin_keep.shape[0]
    scale = scale_of(sum_mine[0:1, 0:1] + sum_theirs[0:1, 0:1], entries)
    scale = jnp.where(core == 0, 1.0, jnp.broadcast_to(scale, (rows, LANES)))
    mine = pltpu.roll(fin_keep[...] * scale, shift, 1)[:, :width]
    theirs = pltpu.roll(fin_recv[...] * scale, shift, 1)[:, :width]
    out[pl.ds(pl.multiple_of(core * rows, rows), rows), :] = mine
    out[pl.ds(pl.multiple_of((1 - core) * rows, rows), rows), :] = theirs


def small_call(kernel, outs, scal, *ins):
    vmem = pltpu.VMEM
    return pl.pallas_call(
        kernel,
        out_shape=outs,
        in_specs=[pl.BlockSpec(memory_space=pltpu.SMEM)] + [pl.BlockSpec(memory_space=vmem)] * len(ins),
        out_specs=[pl.BlockSpec(memory_space=vmem)] * len(outs),
        compiler_params=pltpu.CompilerParams(vmem_limit_bytes=20 * MIB),
    )(scal, *ins)


def batches(rows):
    return [[0], [1], list(range(2, rows))]


def absorb(boundary_in, mpo, proj):
    bond, phys, width = boundary_in.shape[2:]
    n = lax.axis_size("bond")
    sites = lax.axis_size("sites")
    groups = lax.axis_size("rows")
    group_rows = proj.shape[0]
    core = lax.axis_index("rows")
    j = lax.axis_index("bond")
    half = bond // 2
    step = half // n
    entries = bond * phys * bond
    scal = jnp.stack([core, j]).astype(jnp.int32)

    own = proj[:, 0]

    def slices(which):
        got = lax.dynamic_slice_in_dim(own, which * half + j * step, step, 1)
        return jnp.swapaxes(got.reshape(group_rows, step * phys, bond), 1, 2)

    mine = slices(core)
    got = swap_cores(slices(1 - core))

    start = lax.dynamic_slice_in_dim(boundary_in[0, 0], core * half, half, 0)
    pack = LANES // width
    start = start.reshape(pack, half // pack, phys, width)
    start = jnp.concatenate([start[g] for g in range(pack)], axis=-1).reshape(half // pack * phys, LANES)
    pieces = [start] + [from_peer(start, k, n) for k in range(1, n)]

    other = swap_cores(own)
    mpo_own = mpo[:, 0]
    mpo_other = swap_cores(mpo_own)

    flat = (group_rows, bond * phys, bond)
    own_flat, other_flat = (pltpu.with_memory_space_constraint(v.reshape(flat), pltpu.HBM) for v in (own, other))

    def pick(row, own_value, other_value):
        source, slot = divmod(row, group_rows)
        return jnp.where(core == source, own_value[slot], other_value[slot])

    all_rows = range(groups * group_rows)
    mats = jnp.stack([pick(row, mpo_own, mpo_other) for row in all_rows])
    mats = jnp.transpose(mats, (0, 3, 1, 4, 2)).reshape(len(all_rows), phys * phys, phys * phys)
    high = lax.reduce_precision(mats, 8, 7)
    low = (mats - high).astype(bf16)
    high = high.astype(bf16)
    mats = jnp.concatenate([jnp.concatenate([high, high], 2), jnp.concatenate([low, low], 2)], 1)

    ring = [(i, (i + 1) % sites) for i in range(sites)]
    lefts = {}
    for rows in batches(groups * group_rows):
        value = jnp.stack([pick(r, mine, got) for r in rows])
        value = lax.ppermute(value, "sites", ring)
        parts = [value] + [from_peer(value, k, n) for k in range(1, n)]
        for position, r in enumerate(rows):
            lefts[r] = (position, parts)

    keep = recv = None
    for row in all_rows:
        first, stats = row == 0, row == group_rows
        place, parts = lefts[row]
        entry = pieces if first else [keep, recv]
        entry = entry + [own_flat, other_flat, mats]

        def cfg(do_a, do_b):
            return (n, first, stats, do_a, do_b, row, bond, phys, group_rows, place)

        if first:
            (mixed,) = row_call(cfg(True, False), scal, entry)
            keep, send = row_call(cfg(False, True), scal, [mixed] + parts)
        else:
            result = row_call(cfg(True, True), scal, entry + parts)
            keep, send = result[:2]
            if stats:
                full, sum_first = result[2:]
                sum_first_other = swap_cores(sum_first)
        recv = swap_cores(send)
    rows_half = half * phys
    block = jax.ShapeDtypeStruct((rows_half, LANES), f32)
    fin_keep, fin_send, sum_last = small_call(
        functools.partial(sum_kernel, entries, width),
        [block, block, jax.ShapeDtypeStruct((8, LANES), f32)],
        scal, keep, recv, full, sum_first, sum_first_other,
    )
    (out,) = small_call(
        functools.partial(final_kernel, entries, width),
        [jax.ShapeDtypeStruct((bond * phys, width), f32)],
        scal, fin_keep, swap_cores(fin_send), sum_last, swap_cores(sum_last),
    )
    return out.reshape(1, 1, 1, bond, phys, width)


def solution(mesh):
    return jax.shard_map(
        absorb,
        mesh=mesh,
        in_specs=(
            P(None, "sites", None, None, "bond"),
            P("rows", "sites", None, None, None, None),
            P("rows", "sites", None, None, None),
        ),
        out_specs=P("rows", None, "sites", None, None, "bond"),
        check_vma=False,
    )
```
